32 devices in a mesh: snp: 4 (over y, core), ind: 8 (over z, x).
Axes of the slice: x: 2, y: 2, z: 4, core: 2. Of those that a mesh axis runs over, the one named last changes fastest.
Arguments:
- genotypes: bfloat16 [32768, 512], P('ind', 'snp'), as said below
- labels: int32 [32768], P('ind'), may hold values 0 or 1
- offset: float32 [32768], P('ind'), may hold values from -6 to 6
- coefficients: float32 [512], P('snp'), may hold values from -6 to 6, as said below
- penalty: float32 [512], P('snp'), may hold values from 0.02 to 0.5
- breaks: int32 [4], replicated, may hold values 0 or 1
Outputs:
- coef_next: float32 [512], P('snp')
- fitted: float32 [32768], P('ind')
The draws below stay inside these ranges and needn't reach their ends.
Inputs may be any that keep to these rules, and one draw needn't show every extreme that they name: `genotypes`: finite real values. `coefficients`: finite real values.
All inputs are finite; a program needn't handle non-finite values. No bound on the sum of `labels` on one device may be relied on, other than what follows from the above.
Results may differ from the reference program's by a relative error of at most 0.0038.
Values may be sent and summed in bfloat16 or wider, within the bound.
A program may use at most 64 MiB of HBM per device.

```python
import math
import jax
import jax.numpy as jnp
from jax import lax

BLOCK = 128
ITERS = 3
NIND = 32768
NBLK = 4
P_SIZE = 512


def draw_genotypes(key, part):
    noise_key = jax.random.fold_in(key, 0)
    scale_key = jax.random.fold_in(key, 1)
    mix_key = jax.random.fold_in(key, 3)
    kernel_reach = BLOCK
    log_scale = jax.random.uniform(scale_key, (1, P_SIZE), jnp.float32, math.log(0.5), math.log(2.0))
    snp_scale = jnp.exp(log_scale)
    mixing = jax.random.normal(mix_key, (kernel_reach, P_SIZE), jnp.float32) * (1.0 / math.sqrt(kernel_reach))
    piece_count = math.gcd(NIND, 64)
    piece_rows = NIND // piece_count

    def one_piece(piece_index):
        piece_key = jax.random.fold_in(noise_key, piece_index)
        noise_field = jax.random.normal(piece_key, (piece_rows, P_SIZE + kernel_reach - 1), jnp.float32)
        common = jnp.zeros((piece_rows, 1), jnp.float32)
        running_sum = noise_field[:, 0:P_SIZE] * mixing[0:1, :]
        for lag_index in range(1, kernel_reach):
            running_sum = running_sum + noise_field[:, lag_index:lag_index + P_SIZE] * mixing[lag_index:lag_index + 1, :]
        return running_sum * snp_scale + common
    pieces = lax.map(one_piece, jnp.arange(piece_count, dtype=jnp.int32))
    return pieces.reshape(NIND, P_SIZE).astype(jnp.bfloat16)


def draw_coefficients(key, part):
    sign_key, value_key = jax.random.split(jax.random.fold_in(key, 7711), 2)
    block_sign = (jax.random.randint(sign_key, (NBLK, 1), 0, 2) * 2 - 1).astype(jnp.float32)
    spread = jax.random.normal(value_key, (NBLK, BLOCK), jnp.float32)
    values = block_sign * 4.0 + 1.5 * spread
    return jnp.clip(values, -6.0, 6.0).reshape(P_SIZE).astype(jnp.float32)


def plant(drawn, rng, least, high):
    index_at = [jax.random.randint(jax.random.fold_in(rng, axis), (), 0, length) for axis, length in enumerate(drawn.shape)]
    longest = drawn.shape.index(max(drawn.shape))
    beside = index_at[:longest] + [(index_at[longest] + 1) % drawn.shape[longest]] + index_at[longest + 1:]
    return drawn.at[tuple(index_at)].set(least).at[tuple(beside)].set(high)


def shard_levels(rng, shape, shards, least, largest):
    def one(axis_at, parts):
        steps = jax.random.uniform(jax.random.fold_in(jax.random.fold_in(rng, 6), axis_at), (parts,), jnp.float32, least / len(shards), largest / len(shards))
        return jnp.repeat(jnp.exp(steps), shape[axis_at] // parts).reshape((-1,) + (1,) * (len(shape) - axis_at - 1))

    loudness = one(*shards[0])
    for cut in shards[1:]:
        loudness = loudness * one(*cut)
    return loudness


def bell_draw(key, shape, deviation, bound, shards=(), kind=jnp.bfloat16):
    factor_of = shard_levels(key, shape, shards, -0.22, 0.18) if shards else 1.0
    drawn = jax.random.normal(key, shape, jnp.float32) * deviation * factor_of
    return jnp.minimum(jnp.maximum(drawn, -bound), bound).astype(kind)


def setup_inputs(seed: int = 0) -> dict:
    arg_keys = jax.random.split(jax.random.key(seed), 7)
    genotypes = draw_genotypes(jax.random.fold_in(arg_keys[6], 71), 0)
    labels = plant((jax.random.randint(arg_keys[1], (NIND,), 0, 2) < 1).astype(jnp.int32), jax.random.fold_in(arg_keys[1], 1), 0, 1)
    offset = bell_draw(arg_keys[2], (NIND,), 1.0, 6.0, ((0, 8),), jnp.float32)
    coefficients = draw_coefficients(jax.random.fold_in(arg_keys[6], 71), 0)
    penalty = jnp.clip(jnp.exp(math.log(0.5) - 3.218876 * jax.random.uniform(arg_keys[4], (P_SIZE,), jnp.float32) ** shard_levels(arg_keys[4], (P_SIZE,), ((0, 4),), -0.2, 0.2)), 0.02, 0.5)
    breaks = plant((jax.random.randint(arg_keys[5], (NBLK,), 0, 3) < 1).astype(jnp.int32), jax.random.fold_in(arg_keys[5], 1), 0, 1)
    return dict(genotypes=genotypes, labels=labels, offset=offset, coefficients=coefficients, penalty=penalty, breaks=breaks)


def reference(genotypes, labels, offset, coefficients, penalty, breaks):
    inv_root = 1.0 / math.sqrt(NIND)
    highest = lax.Precision.HIGHEST
    contraction = (((0,), (0,)), ((), ()))
    coef_half = coefficients.astype(jnp.bfloat16)
    linear_pred = offset + jnp.dot(genotypes, coef_half, preferred_element_type=jnp.float32) * inv_root
    fitted = jax.nn.sigmoid(linear_pred)
    weights = fitted * (1.0 - fitted)
    residual_half = (labels.astype(jnp.float32) - fitted).astype(jnp.bfloat16)

    def block_terms(block_id):
        own_block = lax.dynamic_slice_in_dim(genotypes, (block_id * BLOCK).astype(jnp.int32), BLOCK, 1)
        later_id = jnp.minimum(block_id + 1, NBLK - 1).astype(jnp.int32)
        next_block = lax.dynamic_slice_in_dim(genotypes, (later_id * BLOCK).astype(jnp.int32), BLOCK, 1)
        weighted = (weights[:, None] * own_block).astype(jnp.bfloat16)
        diag_part = lax.dot_general(weighted, own_block, contraction, preferred_element_type=jnp.float32)
        coupled_part = lax.dot_general(weighted, next_block, contraction, preferred_element_type=jnp.float32)
        score_part = lax.dot_general(own_block, residual_half, contraction, preferred_element_type=jnp.float32)
        return (diag_part, coupled_part, score_part)
    block_ids = jnp.arange(NBLK, dtype=jnp.int32)
    diag_gram, coupling_gram, score = lax.map(block_terms, block_ids)
    pen_blocks = penalty.reshape(NBLK, BLOCK)
    coef_blocks = coefficients.reshape(NBLK, BLOCK)
    curvature = diag_gram / NIND + jnp.eye(BLOCK, dtype=jnp.float32)[None, :, :] * pen_blocks[:, :, None]
    following_break = jnp.concatenate([breaks[1:], jnp.ones((1,), jnp.int32)])
    keep_link = (1 - following_break).astype(jnp.float32)
    right_blocks = coupling_gram / NIND * keep_link[:, None, None]
    left_blocks = jnp.concatenate([jnp.zeros((1, BLOCK, BLOCK), jnp.float32), right_blocks[:-1]], axis=0)
    gradient = score * inv_root - pen_blocks * coef_blocks

    def apply_hessian(vector):
        zero_row = jnp.zeros((1, BLOCK), jnp.float32)
        next_dir = jnp.concatenate([vector[1:], zero_row], axis=0)
        prior_dir = jnp.concatenate([zero_row, vector[:-1]], axis=0)
        return jnp.einsum('bij,bj->bi', curvature, vector, precision=highest) + jnp.einsum('bij,bj->bi', right_blocks, next_dir, precision=highest) + jnp.einsum('bji,bj->bi', left_blocks, prior_dir, precision=highest)
    solution = jnp.zeros((NBLK, BLOCK), jnp.float32)
    residual = gradient
    direction = gradient
    norm_now = jnp.sum(residual * residual)
    for iteration in range(ITERS):
        image = apply_hessian(direction)
        step_length = norm_now / jnp.sum(direction * image)
        solution = solution + step_length * direction
        residual = residual - step_length * image
        if iteration + 1 < ITERS:
            norm_next = jnp.sum(residual * residual)
            direction = residual + norm_next / norm_now * direction
            norm_now = norm_next
    return (coefficients + solution.reshape(-1), fitted)
```

```python
import functools
import math

import jax
import jax.numpy as jnp
from jax import lax
from jax.experimental import pallas as pl
from jax.experimental.pallas import tpu as pltpu
from jax.sharding import PartitionSpec as P

ITERS = 3
BF16 = jnp.bfloat16
F32 = jnp.float32
MESH = pl.DeviceIdType.MESH


def split_rows(vector):
    high = vector.astype(BF16).astype(F32)
    rest = vector - high
    middle = rest.astype(BF16).astype(F32)
    low = rest - middle
    shape = (8, vector.shape[1])
    row = lax.broadcasted_iota(jnp.int32, shape, 0)
    spread = [jnp.broadcast_to(term, shape) for term in (high, middle, low)]
    rows = jnp.where(row == 0, spread[0], jnp.where(row == 1, spread[1], spread[2]))
    return jnp.where(row < 3, rows, 0.0).astype(BF16)


def three(rows):
    return rows[0:1] + rows[1:2] + rows[2:3]


def along_snps(rows, block):
    return lax.dot_general(rows, block, (((1,), (1,)), ((), ())), preferred_element_type=F32)


def along_people(rows, block):
    return lax.dot_general(rows, block, (((1,), (0,)), ((), ())), preferred_element_type=F32)


def kernel(
    snps, inds, people,
    geno_ref, labels_ref, offset_ref, coef_ref, pen_ref, breaks_ref,
    coef_out, fitted_out,
    own, prior, later, etas, part_i, part_s, dirs, images, pens,
    load_sem, bulk_send, bulk_recv, eta_send, eta_recv, i_send, i_recv, s_send, s_recv,
):
    s = lax.axis_index("snp")
    i = lax.axis_index("ind")
    half = own.shape[0] // 2
    width = own.shape[1]
    load = pltpu.make_async_copy(geno_ref, own, load_sem)
    load.start()

    barrier = pltpu.get_barrier_semaphore()
    for step in range(1, snps):
        pl.semaphore_signal(
            barrier, inc=1, device_id={"snp": lax.rem(s + step, snps)}, device_id_type=MESH
        )
    for step in range(1, inds):
        pl.semaphore_signal(
            barrier, inc=1, device_id={"ind": lax.rem(i + step, inds)}, device_id_type=MESH
        )

    @pl.when(s == 0)
    def _():
        prior[...] = jnp.zeros_like(prior)

    @pl.when(s == snps - 1)
    def _():
        later[...] = jnp.zeros_like(later)

    dirs[...] = jnp.zeros_like(dirs)
    load.wait()

    def shared(buffer, axis, me, count, send, recv):
        sends = []
        for step in range(1, count):
            sends.append(
                pltpu.make_async_remote_copy(
                    src_ref=buffer.at[me],
                    dst_ref=buffer.at[me],
                    send_sem=send.at[step],
                    recv_sem=recv.at[me],
                    device_id={axis: lax.rem(me + step, count)},
                    device_id_type=MESH,
                )
            )
        for copy in sends:
            copy.start()

        def arrived():
            for step in range(1, count):
                source = lax.rem(me + count - step, count)
                pltpu.make_async_remote_copy(
                    src_ref=buffer.at[source],
                    dst_ref=buffer.at[source],
                    send_sem=send.at[step],
                    recv_sem=recv.at[source],
                    device_id={axis: source},
                    device_id_type=MESH,
                ).wait_recv()

        return sends, arrived

    pending = []

    coef_rows = jnp.broadcast_to(coef_ref[...].astype(BF16).astype(F32), (8, width)).astype(BF16)
    etas[s] = along_snps(coef_rows, own[...])[0:1]
    pl.semaphore_wait(barrier, snps - 1 + inds - 1)
    sends, arrived = shared(etas, "snp", s, snps, eta_send, eta_recv)
    pending += sends

    to_later = pltpu.make_async_remote_copy(
        src_ref=own.at[pl.ds(half, half)],
        dst_ref=prior,
        send_sem=bulk_send.at[0],
        recv_sem=bulk_recv.at[0],
        device_id={"snp": jnp.minimum(s + 1, snps - 1)},
        device_id_type=MESH,
    )
    to_prior = pltpu.make_async_remote_copy(
        src_ref=own.at[pl.ds(0, half)],
        dst_ref=later,
        send_sem=bulk_send.at[1],
        recv_sem=bulk_recv.at[1],
        device_id={"snp": jnp.maximum(s - 1, 0)},
        device_id_type=MESH,
    )

    @pl.when(s < snps - 1)
    def _():
        to_later.start()

    @pl.when(s > 0)
    def _():
        to_prior.start()

    arrived()
    total = etas[0]
    for block in range(1, snps):
        total = total + etas[block]
    linear_pred = offset_ref[...] + total * (1.0 / math.sqrt(people))
    fitted = 1.0 / (1.0 + jnp.exp(-linear_pred))
    fitted_out[...] = fitted
    weights = fitted * (1.0 - fitted)
    residual_half = (labels_ref[...].astype(F32) - fitted).astype(BF16).astype(F32)
    residual_rows = jnp.broadcast_to(residual_half, (8, 2 * half)).astype(BF16)
    row4 = lax.broadcasted_iota(jnp.int32, (4, width), 0)

    def stacked(first, second, third):
        rows = [jnp.broadcast_to(term, (4, width)) for term in (first, second, third)]
        value = jnp.where(row4 == 0, rows[0], jnp.where(row4 == 1, rows[1], rows[2]))
        return jnp.where(row4 < 3, value, 0.0)

    def summed_inds(turn, value):
        buffer = part_i.at[turn]
        buffer[i] = value
        sends, arrived = shared(buffer, "ind", i, inds, i_send.at[turn], i_recv.at[turn])
        arrived()
        total = buffer[0]
        for other in range(1, inds):
            total = total + buffer[other]
        return total, sends

    def spread_snps(turn, value):
        buffer = part_s.at[turn]
        buffer[s] = value
        sends, arrived = shared(buffer, "snp", s, snps, s_send.at[turn], s_recv.at[turn])
        arrived()
        return buffer, sends

    zero_row = jnp.zeros((1, width), F32)
    score = along_people(residual_rows, own[...])[0:1]
    total, sends = summed_inds(0, stacked(score, zero_row, zero_row))
    pending += sends
    pen = pen_ref[...]
    gradient = total[0:1] * (1.0 / math.sqrt(people)) - pen * coef_ref[...]
    buffer, sends = spread_snps(0, stacked(gradient, pen, zero_row))
    pending += sends
    for block in range(snps):
        images[block : block + 1] = buffer[block][0:1]
        pens[block : block + 1] = buffer[block][1:2]
    residual = images[0:snps]
    penalty = pens[0:snps]

    has_prior = jnp.where(s > 0, 1, 0)
    has_later = jnp.where(s < snps - 1, 1, 0)
    keep_prior = ((1 - breaks_ref[s]) * has_prior).astype(F32)
    keep_later = ((1 - breaks_ref[jnp.minimum(s + 1, snps - 1)]) * has_later).astype(F32)
    weights_a, weights_b = weights[:, :half], weights[:, half:]

    @pl.when(s > 0)
    def _():
        to_later.wait_recv()

    @pl.when(s < snps - 1)
    def _():
        to_prior.wait_recv()

    def whole_sum(value):
        return jnp.sum(jnp.sum(value, axis=1, keepdims=True), axis=0, keepdims=True)

    solution = jnp.zeros_like(residual)
    direction = residual
    norm_now = whole_sum(residual * residual)
    for iteration in range(ITERS):
        turn = iteration + 1
        dirs[1 : snps + 1] = direction
        mine = three(along_snps(split_rows(dirs[pl.ds(s + 1, 1)]), own[...]))
        before = three(along_snps(split_rows(dirs[pl.ds(s, 1)]), prior[...])) * keep_prior
        after = three(along_snps(split_rows(dirs[pl.ds(s + 2, 1)]), later[...])) * keep_later
        mine_a, mine_b = mine[:, :half], mine[:, half:]
        if iteration + 1 < ITERS:
            both_a = weights_a * (mine_a + after)
            both_b = weights_b * (mine_b + before)
            image = three(along_people(split_rows(both_a), own[:half]))
            image = image + three(along_people(split_rows(both_b), own[half:]))
            down = three(along_people(split_rows(weights_b * mine_b * keep_prior), prior[...]))
            up = three(along_people(split_rows(weights_a * mine_a * keep_later), later[...]))
            total, sends = summed_inds(turn, stacked(down, image, up))
            pending += sends
            buffer, sends = spread_snps(turn, total)
            pending += sends
            for block in range(snps):
                value = buffer[block][1:2]
                if block + 1 < snps:
                    value = value + buffer[block + 1][0:1]
                if block > 0:
                    value = value + buffer[block - 1][2:3]
                images[block : block + 1] = value
            image = images[0:snps] * (1.0 / people) + penalty * direction
            product = whole_sum(direction * image)
        else:
            energy = weights_a * mine_a * (mine_a + 2.0 * after)
            energy = energy + weights_b * mine_b * (mine_b + 2.0 * before)
            lanes = energy[:, :width]
            for start in range(width, half, width):
                lanes = lanes + energy[:, start : start + width]
            total, sends = summed_inds(turn, stacked(lanes, zero_row, zero_row))
            pending += sends
            buffer, sends = spread_snps(turn, total)
            pending += sends
            lanes = buffer[0][0:1]
            for block in range(1, snps):
                lanes = lanes + buffer[block][0:1]
            product = jnp.sum(lanes, axis=1, keepdims=True) * (1.0 / people)
            product = product + whole_sum(penalty * direction * direction)
        step_length = norm_now / product
        solution = solution + step_length * direction
        if iteration + 1 < ITERS:
            residual = residual - step_length * image
            norm_next = whole_sum(residual * residual)
            direction = residual + norm_next / norm_now * direction
            norm_now = norm_next

    dirs[1 : snps + 1] = solution
    coef_out[...] = coef_ref[...] + dirs[pl.ds(s + 1, 1)]

    for copy in pending:
        copy.wait_send()

    @pl.when(s < snps - 1)
    def _():
        to_later.wait_send()

    @pl.when(s > 0)
    def _():
        to_prior.wait_send()


def local(snps, inds, genotypes, labels, offset, coefficients, penalty, breaks):
    rows, width = genotypes.shape
    turns = ITERS + 1
    padded = -(-(snps + 2) // 8) * 8
    vmem = pl.BlockSpec(memory_space=pltpu.VMEM)
    dma = pltpu.SemaphoreType.DMA
    coef_next, fitted = pl.pallas_call(
        functools.partial(kernel, snps, inds, rows * inds),
        out_shape=(
            jax.ShapeDtypeStruct((1, width), F32),
            jax.ShapeDtypeStruct((1, rows), F32),
        ),
        in_specs=[
            pl.BlockSpec(memory_space=pl.ANY), vmem, vmem, vmem, vmem,
            pl.BlockSpec(memory_space=pltpu.SMEM),
        ],
        out_specs=(vmem, vmem),
        scratch_shapes=[
            pltpu.VMEM((rows, width), BF16),
            pltpu.VMEM((rows // 2, width), BF16),
            pltpu.VMEM((rows // 2, width), BF16),
            pltpu.VMEM((snps, 1, rows), F32),
            pltpu.VMEM((turns, inds, 4, width), F32),
            pltpu.VMEM((turns, snps, 4, width), F32),
            pltpu.VMEM((padded, width), F32),
            pltpu.VMEM((padded, width), F32),
            pltpu.VMEM((padded, width), F32),
            dma(()),
            dma((2,)),
            dma((2,)),
            dma((snps,)),
            dma((snps,)),
            dma((turns, inds)),
            dma((turns, inds)),
            dma((turns, snps)),
            dma((turns, snps)),
        ],
        compiler_params=pltpu.CompilerParams(
            collective_id=0, has_side_effects=True, vmem_limit_bytes=32 * 1024 * 1024
        ),
    )(
        genotypes,
        labels.reshape(1, rows),
        offset.reshape(1, rows),
        coefficients.reshape(1, width),
        penalty.reshape(1, width),
        breaks,
    )
    return coef_next.reshape(width), fitted.reshape(rows)


def solution(mesh):
    in_specs = (P("ind", "snp"), P("ind"), P("ind"), P("snp"), P("snp"), P())
    out_specs = (P("snp"), P("ind"))
    body = functools.partial(local, mesh.shape["snp"], mesh.shape["ind"])
    return jax.shard_map(body, mesh=mesh, in_specs=in_specs, out_specs=out_specs, check_vma=False)
```

```python
import functools
import math

import jax
import jax.numpy as jnp
from jax import lax
from jax.experimental import pallas as pl
from jax.experimental.pallas import tpu as pltpu
from jax.sharding import PartitionSpec as P

ITERS = 3
BF16 = jnp.bfloat16
F32 = jnp.float32
MESH = pl.DeviceIdType.MESH


def split_rows(vector):
    high = vector.astype(BF16).astype(F32)
    rest = vector - high
    middle = rest.astype(BF16).astype(F32)
    low = rest - middle
    shape = (8, vector.shape[1])
    row = lax.broadcasted_iota(jnp.int32, shape, 0)
    spread = [jnp.broadcast_to(term, shape) for term in (high, middle, low)]
    rows = jnp.where(row == 0, spread[0], jnp.where(row == 1, spread[1], spread[2]))
    return jnp.where(row < 3, rows, 0.0).astype(BF16)


def three(rows):
    return rows[0:1] + rows[1:2] + rows[2:3]


def along_snps(rows, block):
    return lax.dot_general(rows, block, (((1,), (1,)), ((), ())), preferred_element_type=F32)


def along_people(rows, block):
    return lax.dot_general(rows, block, (((1,), (0,)), ((), ())), preferred_element_type=F32)


def kernel(
    snps, inds, people,
    geno_in, labels_in, offset_in, coef_in, pen_in, breaks_in,
    coef_out, fitted_out,
    labels_ref, offset_ref, coef_ref, pen_ref, breaks_ref, own, prior, later, etas, parts, dirs, images, pens,
    load_sem, bulk_send, bulk_recv, eta_send, eta_recv, part_send, part_recv,
):
    s = lax.axis_index("snp")
    i = lax.axis_index("ind")
    half = own.shape[0] // 2
    width = own.shape[1]
    loads = [
        pltpu.make_async_copy(source, target, load_sem.at[slot])
        for slot, (source, target) in enumerate(
            [
                (coef_in, coef_ref),
                (geno_in, own),
                (labels_in, labels_ref),
                (offset_in, offset_ref),
                (pen_in, pen_ref),
                (breaks_in, breaks_ref),
            ]
        )
    ]
    for copy in loads:
        copy.start()

    barrier = pltpu.get_barrier_semaphore()
    devices = snps * inds

    def for_others(act):
        def one(step, carry):
            act((lax.rem(s + step // inds, snps), lax.rem(i + step % inds, inds)), step)
            return carry

        if devices <= 64:
            for step in range(1, devices):
                one(step, 0)
        else:
            lax.fori_loop(1, devices, one, 0)

    for_others(
        lambda other, step: pl.semaphore_signal(
            barrier, inc=1, device_id=other, device_id_type=MESH
        )
    )

    @pl.when(s == 0)
    def _():
        prior[...] = jnp.zeros_like(prior)

    @pl.when(s == snps - 1)
    def _():
        later[...] = jnp.zeros_like(later)

    dirs[...] = jnp.zeros_like(dirs)
    for copy in loads:
        copy.wait()

    def shared(buffer, axis, me, count, send, recv):
        sends = []
        for step in range(1, count):
            sends.append(
                pltpu.make_async_remote_copy(
                    src_ref=buffer.at[me],
                    dst_ref=buffer.at[me],
                    send_sem=send.at[step],
                    recv_sem=recv.at[me],
                    device_id={axis: lax.rem(me + step, count)},
                    device_id_type=MESH,
                )
            )
        for copy in sends:
            copy.start()

        def arrived():
            for step in range(1, count):
                source = lax.rem(me + count - step, count)
                pltpu.make_async_remote_copy(
                    src_ref=buffer.at[source],
                    dst_ref=buffer.at[source],
                    send_sem=send.at[step],
                    recv_sem=recv.at[source],
                    device_id={axis: source},
                    device_id_type=MESH,
                ).wait_recv()

        return sends, arrived

    pending = []

    coef_rows = jnp.broadcast_to(coef_ref[...].astype(BF16).astype(F32), (8, width)).astype(BF16)
    etas[s] = along_snps(coef_rows, own[...])[0:1]
    pl.semaphore_wait(barrier, devices - 1)
    sends, arrived = shared(etas, "snp", s, snps, eta_send, eta_recv)
    pending += sends

    to_later = pltpu.make_async_remote_copy(
        src_ref=own.at[pl.ds(half, half)],
        dst_ref=prior,
        send_sem=bulk_send.at[0],
        recv_sem=bulk_recv.at[0],
        device_id={"snp": jnp.minimum(s + 1, snps - 1)},
        device_id_type=MESH,
    )
    to_prior = pltpu.make_async_remote_copy(
        src_ref=own.at[pl.ds(0, half)],
        dst_ref=later,
        send_sem=bulk_send.at[1],
        recv_sem=bulk_recv.at[1],
        device_id={"snp": jnp.maximum(s - 1, 0)},
        device_id_type=MESH,
    )

    @pl.when(s < snps - 1)
    def _():
        to_later.start()

    @pl.when(s > 0)
    def _():
        to_prior.start()

    arrived()
    total = etas[0]
    for block in range(1, snps):
        total = total + etas[block]
    linear_pred = offset_ref[...] + total * (1.0 / math.sqrt(people))
    fitted = 1.0 / (1.0 + jnp.exp(-linear_pred))
    fitted_out[...] = fitted
    weights = fitted * (1.0 - fitted)
    residual_half = (labels_ref[...].astype(F32) - fitted).astype(BF16).astype(F32)
    residual_rows = jnp.broadcast_to(residual_half, (8, 2 * half)).astype(BF16)
    row4 = lax.broadcasted_iota(jnp.int32, (4, width), 0)

    def stacked(first, second, third):
        rows = [jnp.broadcast_to(term, (4, width)) for term in (first, second, third)]
        value = jnp.where(row4 == 0, rows[0], jnp.where(row4 == 1, rows[1], rows[2]))
        return jnp.where(row4 < 3, value, 0.0)

    def everywhere(turn, value):
        buffer = parts.at[turn]
        mine = s * inds + i
        buffer[mine] = value

        def send(other, step):
            pltpu.make_async_remote_copy(
                src_ref=buffer.at[mine],
                dst_ref=buffer.at[mine],
                send_sem=part_send.at[turn],
                recv_sem=part_recv.at[turn],
                device_id=other,
                device_id_type=MESH,
            ).start()

        for_others(send)
        received(turn).wait_recv()
        return [jnp.sum(buffer[b * inds : (b + 1) * inds], axis=0) for b in range(snps)]

    def received(turn):
        others = parts.at[turn, pl.ds(0, devices - 1)]
        return pltpu.make_async_remote_copy(
            src_ref=others,
            dst_ref=others,
            send_sem=part_send.at[turn],
            recv_sem=part_recv.at[turn],
            device_id=(lax.rem(s + 1, snps), i),
            device_id_type=MESH,
        )

    zero_row = jnp.zeros((1, width), F32)
    score = along_people(residual_rows, own[...])[0:1]
    scale = jnp.where(i == 0, 1.0, 0.0)
    sums = everywhere(0, stacked(score, pen_ref[...] * scale, coef_ref[...] * scale))
    for block in range(snps):
        score, pen, coef = (sums[block][row : row + 1] for row in range(3))
        images[block : block + 1] = score * (1.0 / math.sqrt(people)) - pen * coef
        pens[block : block + 1] = pen
    residual = images[0:snps]
    penalty = pens[0:snps]

    has_prior = jnp.where(s > 0, 1, 0)
    has_later = jnp.where(s < snps - 1, 1, 0)
    keep_prior = ((1 - breaks_ref[s]) * has_prior).astype(F32)
    keep_later = ((1 - breaks_ref[jnp.minimum(s + 1, snps - 1)]) * has_later).astype(F32)
    weights_a, weights_b = weights[:, :half], weights[:, half:]

    @pl.when(s > 0)
    def _():
        to_later.wait_recv()

    @pl.when(s < snps - 1)
    def _():
        to_prior.wait_recv()

    def whole_sum(value):
        return jnp.sum(jnp.sum(value, axis=1, keepdims=True), axis=0, keepdims=True)

    solution = jnp.zeros_like(residual)
    direction = residual
    norm_now = whole_sum(residual * residual)
    for iteration in range(ITERS):
        turn = iteration + 1
        dirs[1 : snps + 1] = direction
        mine = three(along_snps(split_rows(dirs[pl.ds(s + 1, 1)]), own[...]))
        before = three(along_snps(split_rows(dirs[pl.ds(s, 1)]), prior[...])) * keep_prior
        after = three(along_snps(split_rows(dirs[pl.ds(s + 2, 1)]), later[...])) * keep_later
        mine_a, mine_b = mine[:, :half], mine[:, half:]
        if iteration + 1 < ITERS:
            both_a = weights_a * (mine_a + after)
            both_b = weights_b * (mine_b + before)
            image = three(along_people(split_rows(both_a), own[:half]))
            image = image + three(along_people(split_rows(both_b), own[half:]))
            down = three(along_people(split_rows(weights_b * mine_b * keep_prior), prior[...]))
            up = three(along_people(split_rows(weights_a * mine_a * keep_later), later[...]))
            sums = everywhere(turn, stacked(down, image, up))
            for block in range(snps):
                value = sums[block][1:2]
                if block + 1 < snps:
                    value = value + sums[block + 1][0:1]
                if block > 0:
                    value = value + sums[block - 1][2:3]
                images[block : block + 1] = value
            image = images[0:snps] * (1.0 / people) + penalty * direction
            product = whole_sum(direction * image)
        else:
            energy = weights_a * mine_a * (mine_a + 2.0 * after)
            energy = energy + weights_b * mine_b * (mine_b + 2.0 * before)
            lanes = energy[:, :width]
            for start in range(width, half, width):
                lanes = lanes + energy[:, start : start + width]
            sums = everywhere(turn, stacked(lanes, zero_row, zero_row))
            lanes = sums[0][0:1]
            for block in range(1, snps):
                lanes = lanes + sums[block][0:1]
            product = jnp.sum(lanes, axis=1, keepdims=True) * (1.0 / people)
            product = product + whole_sum(penalty * direction * direction)
        step_length = norm_now / product
        solution = solution + step_length * direction
        if iteration + 1 < ITERS:
            residual = residual - step_length * image
            norm_next = whole_sum(residual * residual)
            direction = residual + norm_next / norm_now * direction
            norm_now = norm_next

    dirs[1 : snps + 1] = solution
    coef_out[...] = coef_ref[...] + dirs[pl.ds(s + 1, 1)]

    for copy in pending:
        copy.wait_send()
    for turn in range(ITERS + 1):
        received(turn).wait_send()

    @pl.when(s < snps - 1)
    def _():
        to_later.wait_send()

    @pl.when(s > 0)
    def _():
        to_prior.wait_send()


def local(snps, inds, genotypes, labels, offset, coefficients, penalty, breaks):
    rows, width = genotypes.shape
    turns = ITERS + 1
    padded = -(-(snps + 2) // 8) * 8
    vmem = pl.BlockSpec(memory_space=pltpu.VMEM)
    dma = pltpu.SemaphoreType.DMA
    coef_next, fitted = pl.pallas_call(
        functools.partial(kernel, snps, inds, rows * inds),
        out_shape=(
            jax.ShapeDtypeStruct((1, width), F32),
            jax.ShapeDtypeStruct((1, rows), F32),
        ),
        in_specs=[pl.BlockSpec(memory_space=pl.ANY)] * 6,
        out_specs=(vmem, vmem),
        scratch_shapes=[
            pltpu.VMEM((1, rows), jnp.int32),
            pltpu.VMEM((1, rows), F32),
            pltpu.VMEM((1, width), F32),
            pltpu.VMEM((1, width), F32),
            pltpu.SMEM(breaks.shape, jnp.int32),
            pltpu.VMEM((rows, width), BF16),
            pltpu.VMEM((rows // 2, width), BF16),
            pltpu.VMEM((rows // 2, width), BF16),
            pltpu.VMEM((snps, 1, rows), F32),
            pltpu.VMEM((turns, snps * inds, 4, width), F32),
            pltpu.VMEM((padded, width), F32),
            pltpu.VMEM((padded, width), F32),
            pltpu.VMEM((padded, width), F32),
            dma((6,)),
            dma((2,)),
            dma((2,)),
            dma((snps,)),
            dma((snps,)),
            dma((turns,)),
            dma((turns,)),
        ],
        compiler_params=pltpu.CompilerParams(
            collective_id=0, has_side_effects=True, vmem_limit_bytes=60 * 1024 * 1024
        ),
    )(
        genotypes,
        labels.reshape(1, rows),
        offset.reshape(1, rows),
        coefficients.reshape(1, width),
        penalty.reshape(1, width),
        breaks,
    )
    return coef_next.reshape(width), fitted.reshape(rows)


def solution(mesh):
    in_specs = (P("ind", "snp"), P("ind"), P("ind"), P("snp"), P("snp"), P())
    out_specs = (P("snp"), P("ind"))
    body = functools.partial(local, mesh.shape["snp"], mesh.shape["ind"])
    return jax.shard_map(body, mesh=mesh, in_specs=in_specs, out_specs=out_specs, check_vma=False)
```

```python
import functools
import math

import jax
import jax.numpy as jnp
from jax import lax
from jax.experimental import pallas as pl
from jax.experimental.pallas import tpu as pltpu
from jax.sharding import PartitionSpec as P

ITERS = 3
BF16 = jnp.bfloat16
F32 = jnp.float32
MESH = pl.DeviceIdType.MESH


def split_rows(vector):
    high = vector.astype(BF16).astype(F32)
    rest = vector - high
    middle = rest.astype(BF16).astype(F32)
    low = rest - middle
    shape = (8, vector.shape[1])
    row = lax.broadcasted_iota(jnp.int32, shape, 0)
    spread = [jnp.broadcast_to(term, shape) for term in (high, middle, low)]
    rows = jnp.where(row == 0, spread[0], jnp.where(row == 1, spread[1], spread[2]))
    return jnp.where(row < 3, rows, 0.0).astype(BF16)


def three(rows):
    return rows[0:1] + rows[1:2] + rows[2:3]


def along_snps(rows, block):
    return lax.dot_general(rows, block, (((1,), (1,)), ((), ())), preferred_element_type=F32)


def along_people(rows, block):
    return lax.dot_general(rows, block, (((1,), (0,)), ((), ())), preferred_element_type=F32)


def kernel(
    snps, inds, people,
    geno_in, labels_in, offset_in, coef_in, pen_in, breaks_in,
    coef_out, fitted_out,
    labels_ref, offset_ref, coef_ref, pen_ref, breaks_ref, own, prior, later, etas, parts, dirs, images, pens,
    load_sem, bulk_send, bulk_recv, eta_send, eta_recv, part_send, part_recv,
):
    s = lax.axis_index("snp")
    i = lax.axis_index("ind")
    half = own.shape[0] // 2
    width = own.shape[1]
    barrier = pltpu.get_barrier_semaphore()
    devices = snps * inds

    def for_others(act):
        def one(step, carry):
            act((lax.rem(s + step // inds, snps), lax.rem(i + step % inds, inds)), step)
            return carry

        if devices <= 64:
            for step in range(1, devices):
                one(step, 0)
        else:
            lax.fori_loop(1, devices, one, 0)

    for_others(
        lambda other, step: pl.semaphore_signal(
            barrier, inc=1, device_id=other, device_id_type=MESH
        )
    )

    loads = [
        pltpu.make_async_copy(source, target, load_sem.at[slot])
        for slot, (source, target) in enumerate(
            [
                (coef_in, coef_ref),
                (geno_in, own),
                (labels_in, labels_ref),
                (offset_in, offset_ref),
                (pen_in, pen_ref),
                (breaks_in, breaks_ref),
            ]
        )
    ]
    for copy in loads:
        copy.start()

    @pl.when(s == 0)
    def _():
        prior[...] = jnp.zeros_like(prior)

    @pl.when(s == snps - 1)
    def _():
        later[...] = jnp.zeros_like(later)

    dirs[...] = jnp.zeros_like(dirs)
    for copy in loads:
        copy.wait()

    def shared(buffer, axis, me, count, send, recv):
        sends = []
        for step in range(1, count):
            sends.append(
                pltpu.make_async_remote_copy(
                    src_ref=buffer.at[me],
                    dst_ref=buffer.at[me],
                    send_sem=send.at[step],
                    recv_sem=recv.at[me],
                    device_id={axis: lax.rem(me + step, count)},
                    device_id_type=MESH,
                )
            )
        for copy in sends:
            copy.start()

        def arrived():
            for step in range(1, count):
                source = lax.rem(me + count - step, count)
                pltpu.make_async_remote_copy(
                    src_ref=buffer.at[source],
                    dst_ref=buffer.at[source],
                    send_sem=send.at[step],
                    recv_sem=recv.at[source],
                    device_id={axis: source},
                    device_id_type=MESH,
                ).wait_recv()

        return sends, arrived

    pending = []

    coef_rows = jnp.broadcast_to(coef_ref[...].astype(BF16).astype(F32), (8, width)).astype(BF16)
    etas[s] = along_snps(coef_rows, own[...])[0:1]
    pl.semaphore_wait(barrier, devices - 1)
    sends, arrived = shared(etas, "snp", s, snps, eta_send, eta_recv)
    pending += sends

    to_later = pltpu.make_async_remote_copy(
        src_ref=own.at[pl.ds(half, half)],
        dst_ref=prior,
        send_sem=bulk_send.at[0],
        recv_sem=bulk_recv.at[0],
        device_id={"snp": jnp.minimum(s + 1, snps - 1)},
        device_id_type=MESH,
    )
    to_prior = pltpu.make_async_remote_copy(
        src_ref=own.at[pl.ds(0, half)],
        dst_ref=later,
        send_sem=bulk_send.at[1],
        recv_sem=bulk_recv.at[1],
        device_id={"snp": jnp.maximum(s - 1, 0)},
        device_id_type=MESH,
    )

    @pl.when(s < snps - 1)
    def _():
        to_later.start()

    @pl.when(s > 0)
    def _():
        to_prior.start()

    arrived()
    total = etas[0]
    for block in range(1, snps):
        total = total + etas[block]
    linear_pred = offset_ref[...] + total * (1.0 / math.sqrt(people))
    fitted = 1.0 / (1.0 + jnp.exp(-linear_pred))
    fitted_out[...] = fitted
    weights = fitted * (1.0 - fitted)
    residual_half = (labels_ref[...].astype(F32) - fitted).astype(BF16).astype(F32)
    residual_rows = jnp.broadcast_to(residual_half, (8, 2 * half)).astype(BF16)
    row4 = lax.broadcasted_iota(jnp.int32, (4, width), 0)

    def stacked(first, second, third):
        rows = [jnp.broadcast_to(term, (4, width)) for term in (first, second, third)]
        value = jnp.where(row4 == 0, rows[0], jnp.where(row4 == 1, rows[1], rows[2]))
        return jnp.where(row4 < 3, value, 0.0)

    def everywhere(turn, value):
        buffer = parts.at[turn]
        mine = s * inds + i
        buffer[mine] = value

        def send(other, step):
            pltpu.make_async_remote_copy(
                src_ref=buffer.at[mine],
                dst_ref=buffer.at[mine],
                send_sem=part_send.at[turn],
                recv_sem=part_recv.at[turn],
                device_id=other,
                device_id_type=MESH,
            ).start()

        for_others(send)
        received(turn).wait_recv()
        return [jnp.sum(buffer[b * inds : (b + 1) * inds], axis=0) for b in range(snps)]

    def received(turn):
        others = parts.at[turn, pl.ds(0, devices - 1)]
        return pltpu.make_async_remote_copy(
            src_ref=others,
            dst_ref=others,
            send_sem=part_send.at[turn],
            recv_sem=part_recv.at[turn],
            device_id=(lax.rem(s + 1, snps), i),
            device_id_type=MESH,
        )

    zero_row = jnp.zeros((1, width), F32)
    score = along_people(residual_rows, own[...])[0:1]
    scale = jnp.where(i == 0, 1.0, 0.0)
    sums = everywhere(0, stacked(score, pen_ref[...] * scale, coef_ref[...] * scale))
    for block in range(snps):
        score, pen, coef = (sums[block][row : row + 1] for row in range(3))
        images[block : block + 1] = score * (1.0 / math.sqrt(people)) - pen * coef
        pens[block : block + 1] = pen
    residual = images[0:snps]
    penalty = pens[0:snps]

    has_prior = jnp.where(s > 0, 1, 0)
    has_later = jnp.where(s < snps - 1, 1, 0)
    keep_prior = ((1 - breaks_ref[s]) * has_prior).astype(F32)
    keep_later = ((1 - breaks_ref[jnp.minimum(s + 1, snps - 1)]) * has_later).astype(F32)
    weights_a, weights_b = weights[:, :half], weights[:, half:]

    @pl.when(s > 0)
    def _():
        to_later.wait_recv()

    @pl.when(s < snps - 1)
    def _():
        to_prior.wait_recv()

    def whole_sum(value):
        return jnp.sum(jnp.sum(value, axis=1, keepdims=True), axis=0, keepdims=True)

    solution = jnp.zeros_like(residual)
    direction = residual
    norm_now = whole_sum(residual * residual)
    for iteration in range(ITERS):
        turn = iteration + 1
        dirs[1 : snps + 1] = direction
        mine = three(along_snps(split_rows(dirs[pl.ds(s + 1, 1)]), own[...]))
        before = three(along_snps(split_rows(dirs[pl.ds(s, 1)]), prior[...])) * keep_prior
        after = three(along_snps(split_rows(dirs[pl.ds(s + 2, 1)]), later[...])) * keep_later
        mine_a, mine_b = mine[:, :half], mine[:, half:]
        if iteration + 1 < ITERS:
            both_a = weights_a * (mine_a + after)
            both_b = weights_b * (mine_b + before)
            image = three(along_people(split_rows(both_a), own[:half]))
            image = image + three(along_people(split_rows(both_b), own[half:]))
            down = three(along_people(split_rows(weights_b * mine_b * keep_prior), prior[...]))
            up = three(along_people(split_rows(weights_a * mine_a * keep_later), later[...]))
            sums = everywhere(turn, stacked(down, image, up))
            for block in range(snps):
                value = sums[block][1:2]
                if block + 1 < snps:
                    value = value + sums[block + 1][0:1]
                if block > 0:
                    value = value + sums[block - 1][2:3]
                images[block : block + 1] = value
            image = images[0:snps] * (1.0 / people) + penalty * direction
            product = whole_sum(direction * image)
        else:
            energy = weights_a * mine_a * (mine_a + 2.0 * after)
            energy = energy + weights_b * mine_b * (mine_b + 2.0 * before)
            lanes = energy[:, :width]
            for start in range(width, half, width):
                lanes = lanes + energy[:, start : start + width]
            sums = everywhere(turn, stacked(lanes, zero_row, zero_row))
            lanes = sums[0][0:1]
            for block in range(1, snps):
                lanes = lanes + sums[block][0:1]
            product = jnp.sum(lanes, axis=1, keepdims=True) * (1.0 / people)
            product = product + whole_sum(penalty * direction * direction)
        step_length = norm_now / product
        solution = solution + step_length * direction
        if iteration + 1 < ITERS:
            residual = residual - step_length * image
            norm_next = whole_sum(residual * residual)
            direction = residual + norm_next / norm_now * direction
            norm_now = norm_next

    dirs[1 : snps + 1] = solution
    coef_out[...] = coef_ref[...] + dirs[pl.ds(s + 1, 1)]

    for copy in pending:
        copy.wait_send()
    for turn in range(ITERS + 1):
        received(turn).wait_send()

    @pl.when(s < snps - 1)
    def _():
        to_later.wait_send()

    @pl.when(s > 0)
    def _():
        to_prior.wait_send()


def local(snps, inds, genotypes, labels, offset, coefficients, penalty, breaks):
    rows, width = genotypes.shape
    turns = ITERS + 1
    padded = -(-(snps + 2) // 8) * 8
    vmem = pl.BlockSpec(memory_space=pltpu.VMEM)
    dma = pltpu.SemaphoreType.DMA
    coef_next, fitted = pl.pallas_call(
        functools.partial(kernel, snps, inds, rows * inds),
        out_shape=(
            jax.ShapeDtypeStruct((1, width), F32),
            jax.ShapeDtypeStruct((1, rows), F32),
        ),
        in_specs=[pl.BlockSpec(memory_space=pltpu.HBM)] * 6,
        out_specs=(vmem, vmem),
        scratch_shapes=[
            pltpu.VMEM((1, rows), jnp.int32),
            pltpu.VMEM((1, rows), F32),
            pltpu.VMEM((1, width), F32),
            pltpu.VMEM((1, width), F32),
            pltpu.SMEM(breaks.shape, jnp.int32),
            pltpu.VMEM((rows, width), BF16),
            pltpu.VMEM((rows // 2, width), BF16),
            pltpu.VMEM((rows // 2, width), BF16),
            pltpu.VMEM((snps, 1, rows), F32),
            pltpu.VMEM((turns, snps * inds, 4, width), F32),
            pltpu.VMEM((padded, width), F32),
            pltpu.VMEM((padded, width), F32),
            pltpu.VMEM((padded, width), F32),
            dma((6,)),
            dma((2,)),
            dma((2,)),
            dma((snps,)),
            dma((snps,)),
            dma((turns,)),
            dma((turns,)),
        ],
        compiler_params=pltpu.CompilerParams(
            collective_id=0, has_side_effects=True, vmem_limit_bytes=16 * 1024 * 1024
        ),
    )(
        *[
            pltpu.with_memory_space_constraint(array, pltpu.HBM)
            for array in (
                genotypes,
                labels.reshape(1, rows),
                offset.reshape(1, rows),
                coefficients.reshape(1, width),
                penalty.reshape(1, width),
                breaks,
            )
        ]
    )
    return coef_next.reshape(width), fitted.reshape(rows)


def solution(mesh):
    in_specs = (P("ind", "snp"), P("ind"), P("ind"), P("snp"), P("snp"), P())
    out_specs = (P("snp"), P("ind"))
    body = functools.partial(local, mesh.shape["snp"], mesh.shape["ind"])
    return jax.shard_map(body, mesh=mesh, in_specs=in_specs, out_specs=out_specs, check_vma=False)
```
